32 devices in a mesh: rows: 8 (over y, x, core), tp: 4 (over z).
Axes of the slice: x: 2, y: 2, z: 4, core: 2. Of those that a mesh axis runs over, the one named last changes fastest.
Arguments:
- inputs: bfloat16 [16384, 768], P(('rows', 'tp')), may hold values from -6 to 6
- segments: int32 [16, 1024], P('rows'), may hold values from 0 to 3, never falling along the last dimension, each value on 1 to 512 neighbouring positions
- row_length: int32 [16], P('rows'), may hold values from 1 to 1024, 12288 in all
- query_weight: bfloat16 [768, 768], P(None, 'tp'), may hold values from -0.21875 to 0.21875
- query_bias: float32 [768], P('tp'), may hold values from -3 to 3
- key_weight: bfloat16 [768, 768], P(None, 'tp'), may hold values from -0.21875 to 0.21875
- value_weight: bfloat16 [768, 768], P(None, 'tp'), may hold values from -0.21875 to 0.21875
- value_bias: float32 [768], P('tp'), may hold values from -3 to 3
- output_weight: bfloat16 [768, 768], P('tp'), may hold values from -0.875 to 0.875
- output_bias: float32 [768], replicated, may hold values from -3 to 3
- attn_gain: float32 [768], replicated, may hold values from 0.5 to 1.5
- attn_shift: float32 [768], replicated, may hold values from -3 to 3
- up_weight: bfloat16 [768, 3072], P(None, 'tp'), may hold values from -0.21875 to 0.21875
- up_bias: float32 [3072], P('tp'), may hold values from -3 to 3
- down_weight: bfloat16 [3072, 768], P('tp'), may hold values from -0.109375 to 0.109375
- down_bias: float32 [768], replicated, may hold values from -3 to 3
- ffn_gain: float32 [768], replicated, may hold values from 0.5 to 1.5
- ffn_shift: float32 [768], replicated, may hold values from -3 to 3
- cotangent: bfloat16 [16384, 768], P(('rows', 'tp')), may hold values from -6 to 6
Outputs:
- layer_out: bfloat16 [16384, 768], P(('rows', 'tp'))
- input_grad: float32 [16384, 768], P(('rows', 'tp'))
- query_weight_grad: float32 [768, 768], P(None, 'tp')
- query_bias_grad: float32 [768], P('tp')
- key_weight_grad: float32 [768, 768], P(None, 'tp')
- value_weight_grad: float32 [768, 768], P(None, 'tp')
- value_bias_grad: float32 [768], P('tp')
- output_weight_grad: float32 [768, 768], P('tp')
- output_bias_grad: float32 [768], replicated
- attn_gain_grad: float32 [768], replicated
- attn_shift_grad: float32 [768], replicated
- up_weight_grad: float32 [768, 3072], P(None, 'tp')
- up_bias_grad: float32 [3072], P('tp')
- down_weight_grad: float32 [3072, 768], P('tp')
- down_bias_grad: float32 [768], replicated
- ffn_gain_grad: float32 [768], replicated
- ffn_shift_grad: float32 [768], replicated
The draws below stay inside these ranges and needn't reach their ends.
Inputs may be any that keep to these rules, and one draw needn't show every extreme that they name: Within each row, segment numbers never fall and each of the 4 segments covers 1 to 512 positions. `row_length`: some row is live over all 1024 tokens.
All inputs are finite; a program needn't handle non-finite values. No bound on the sum of `row_length` on one device may be relied on, other than what follows from the above.
Results may differ from the reference program's by a relative error of at most 0.028.
Values may be sent and summed in bfloat16 or wider, within the bound.
No kernel may reach another device: no remote copies, remote signals or barrier semaphores. Data moves between devices by JAX's collectives and lax.ppermute only.
A program may use at most 128 MiB of HBM per device.

```python
import math
import jax
import jax.numpy as jnp
import numpy as np
from jax import lax

D = 768
HEADS = 12
HD = 64
FF = 3072
LEN = 1024
SEGS = 4
SEQ_DEV = 2
ROWS = 16
TOKENS = 16384
N_TP = 4


def shard_levels(own_key, extent, split, low, largest):
    def one(dim, parts):
        heights = jax.random.uniform(jax.random.fold_in(jax.random.fold_in(own_key, 6), dim), (parts,), jnp.float32, low / len(split), largest / len(split))
        return jnp.repeat(jnp.exp(heights), extent[dim] // parts).reshape((-1,) + (1,) * (len(extent) - dim - 1))

    loudness = one(*split[0])
    for cut in split[1:]:
        loudness = loudness * one(*cut)
    return loudness


def length_profile(number_of, total, reach, skew):
    portions = [(1 << 20) // math.isqrt(rank ** skew) + 1 for rank in range(2, number_of + 1)]
    surplus, holding = total - reach - (number_of - 1), [1] * (number_of - 1)
    while surplus > 0:
        movable = [i for i in range(number_of - 1) if holding[i] < reach]
        whole, budget = sum([portions[i] for i in movable]), surplus
        for i in movable:
            extra = min(reach - holding[i], max(1, budget * portions[i] // whole), surplus)
            holding[i] = holding[i] + extra
            surplus = surplus - extra
    return np.array([reach] + holding)


def uneven(key, number_of, total, most, slope):
    if number_of == 2:
        one = jax.random.randint(key, (), max(1, total - most), min(most, total - 1) + 1)
        return jnp.stack([one, total - one])
    lengths = jnp.asarray(length_profile(number_of, total, most, slope), jnp.int32)
    couples = (number_of - 1) // 2
    giver, sink = lengths[1:1 + 2 * couples:2], lengths[2:2 + 2 * couples:2]
    margin = jnp.minimum(giver - 1, most - sink)
    passed = jax.random.randint(jax.random.fold_in(key, 1), (couples,), 0, 1 << 20) % (margin + 1)
    lengths = lengths.at[1:1 + 2 * couples:2].set(giver - passed).at[2:2 + 2 * couples:2].set(sink + passed)
    return lengths[jax.random.permutation(jax.random.fold_in(key, 2), number_of)]


def normal_values(own_key, dims, deviation, bound, pieces=(), kind=jnp.bfloat16):
    factor_of = shard_levels(own_key, dims, pieces, -0.22, 0.18) if pieces else 1.0
    drawn = jax.random.normal(own_key, dims, jnp.float32) * deviation * factor_of
    return jnp.minimum(jnp.maximum(drawn, -bound), bound).astype(kind)


def setup_inputs(seed: int = 0) -> dict:
    key_list = jax.random.split(jax.random.key(seed), 20)
    return {
        "inputs": normal_values(key_list[0], (TOKENS, D), 1.0, 6.0, ((0, 32),)),
        "segments": jax.vmap(lambda own: jnp.searchsorted(jnp.cumsum(uneven(own, SEGS, LEN, LEN // 2, 1)), jnp.arange(LEN), side="right"))(jax.random.split(key_list[1], ROWS)).reshape((ROWS, LEN)).astype(jnp.int32),
        "row_length": uneven(key_list[2], ROWS, ROWS * LEN * 3 // 4, LEN, 2).astype(jnp.int32),
        "query_weight": normal_values(key_list[3], (D, D), D ** -0.5, 0.21875, ((1, 4),)),
        "query_bias": normal_values(key_list[4], (D,), 0.5, 3.0, ((0, 4),), jnp.float32),
        "key_weight": normal_values(key_list[5], (D, D), D ** -0.5, 0.21875, ((1, 4),)),
        "value_weight": normal_values(key_list[6], (D, D), D ** -0.5, 0.21875, ((1, 4),)),
        "value_bias": normal_values(key_list[7], (D,), 0.5, 3.0, ((0, 4),), jnp.float32),
        "output_weight": normal_values(key_list[8], (D, D), (D // 16) ** -0.5, 0.875, ((0, 4),)),
        "output_bias": normal_values(key_list[9], (D,), 0.5, 3.0, (), jnp.float32),
        "attn_gain": jnp.clip(1.0 + 0.1 * jax.random.normal(key_list[10], (D,), jnp.float32), 0.5, 1.5),
        "attn_shift": normal_values(key_list[11], (D,), 0.5, 3.0, (), jnp.float32),
        "up_weight": normal_values(key_list[12], (D, FF), D ** -0.5, 0.21875, ((1, 4),)),
        "up_bias": normal_values(key_list[13], (FF,), 0.5, 3.0, ((0, 4),), jnp.float32),
        "down_weight": normal_values(key_list[14], (FF, D), FF ** -0.5, 0.109375, ((0, 4),)),
        "down_bias": normal_values(key_list[15], (D,), 0.5, 3.0, (), jnp.float32),
        "ffn_gain": jnp.clip(1.0 + 0.1 * jax.random.normal(key_list[16], (D,), jnp.float32), 0.5, 1.5),
        "ffn_shift": normal_values(key_list[17], (D,), 0.5, 3.0, (), jnp.float32),
        "cotangent": normal_values(key_list[18], (TOKENS, D), 1.0, 6.0, ((0, 32),)),
    }


EPS = 1e-12
highest = lax.Precision.HIGHEST

@jax.custom_vjp
def low(v):
    return lax.optimization_barrier(v.astype(jnp.bfloat16)).astype(jnp.float32)

@jax.custom_vjp
def low_back(v):
    return v

def low_keep(v):
    return (low(v), None)

def low_pass(kept, grad):
    return (grad,)

def back_keep(v):
    return (v, None)

def back_low(kept, grad):
    return (low(grad),)
low.defvjp(low_keep, low_pass)
low_back.defvjp(back_keep, back_low)

def layer_norm(values, scale_gain, offset):
    centre = values - lax.optimization_barrier(jnp.mean(values, axis=-1, keepdims=True))
    inverse = lax.rsqrt(lax.optimization_barrier(jnp.mean(centre * centre, axis=-1, keepdims=True)) + EPS)
    return centre * inverse * scale_gain + offset

def allowed_mask(seg_row, length):
    places = jnp.arange(seg_row.shape[0], dtype=jnp.int32)
    matching = seg_row[:, None] == seg_row[None, :]
    live_keys = (places < length)[None, :]
    return matching & live_keys | (places[:, None] == places[None, :])

def attend_sequence(packed):
    queries, keys_all, values_all, seg_row, length = packed
    raw_scores = low_back(jnp.einsum('qhd,khd->hqk', queries, keys_all, precision=highest))
    scores = jnp.where(allowed_mask(seg_row, length)[None], raw_scores * HD ** (-0.5), -1e+30)
    row_max = lax.optimization_barrier(jnp.max(scores, axis=-1, keepdims=True))
    exponent = jnp.exp(scores - row_max)
    probabilities = low(exponent / lax.optimization_barrier(jnp.sum(exponent, axis=-1, keepdims=True)))
    return jnp.einsum('hqk,khd->qhd', probabilities, values_all, precision=highest)

def column_groups(matrix):
    return matrix.reshape(matrix.shape[0], N_TP, -1).transpose(1, 0, 2)

def row_groups(matrix):
    return matrix.reshape(N_TP, -1, matrix.shape[1])

def widen(values):
    return low_back(jnp.broadcast_to(values[None], (N_TP,) + values.shape))

def layer(block_in, params, block_seg, block_len):
    query_weight, query_bias, key_weight, value_weight, value_bias, output_weight, output_bias, attn_gain, attn_shift, up_weight, up_bias, down_weight, down_bias, ffn_gain, ffn_shift = params
    tokens_here = block_in.shape[0]
    seqs_here = block_seg.shape[0]
    spread_in = widen(block_in)

    def heads_of(matrix, bias_vec):
        projected = jnp.einsum('gtd,gde->gte', spread_in, column_groups(matrix), precision=highest)
        projected = low_back(low(projected + bias_vec.reshape(N_TP, 1, -1)))
        return projected.transpose(1, 0, 2).reshape(seqs_here, LEN, HEADS, HD)
    queries = heads_of(query_weight, query_bias)
    keys_all = heads_of(key_weight, jnp.zeros_like(query_bias))
    values_all = heads_of(value_weight, value_bias)
    context = lax.map(jax.checkpoint(attend_sequence), (queries, keys_all, values_all, block_seg, block_len))
    context = low_back(low(context.reshape(tokens_here, N_TP, -1)))
    attn_parts = jnp.einsum('tge,ged->gtd', context, row_groups(output_weight), precision=highest)
    attn_out = lax.optimization_barrier(jnp.sum(low_back(low(attn_parts)), axis=0)) + output_bias
    hidden_mid = layer_norm(block_in + attn_out, attn_gain, attn_shift)
    spread_mid = widen(low(hidden_mid))
    pre_act = low_back(jnp.einsum('gtd,gdf->gtf', spread_mid, column_groups(up_weight), precision=highest))
    pre_act = pre_act + up_bias.reshape(N_TP, 1, -1)
    activated = low(jax.nn.gelu(pre_act, approximate=False))
    ffn_parts = jnp.einsum('gtf,gfd->gtd', activated, row_groups(down_weight), precision=highest)
    ffn_out = lax.optimization_barrier(jnp.sum(low_back(low(ffn_parts)), axis=0)) + down_bias
    return layer_norm(hidden_mid + ffn_out, ffn_gain, ffn_shift)

def reference(inputs, segments, row_length, query_weight, query_bias, key_weight, value_weight, value_bias, output_weight, output_bias, attn_gain, attn_shift, up_weight, up_bias, down_weight, down_bias, ffn_gain, ffn_shift, cotangent):
    params = tuple((tensor.astype(jnp.float32) for tensor in (query_weight, query_bias, key_weight, value_weight, value_bias, output_weight, output_bias, attn_gain, attn_shift, up_weight, up_bias, down_weight, down_bias, ffn_gain, ffn_shift)))
    block_count = ROWS // SEQ_DEV
    block_span = SEQ_DEV * LEN
    block_inputs = inputs.astype(jnp.float32).reshape(block_count, block_span, D)
    block_cots = cotangent.astype(jnp.float32).reshape(block_count, block_span, D)
    block_segs = segments.reshape(block_count, SEQ_DEV, LEN)
    block_lens = row_length.reshape(block_count, SEQ_DEV)

    def advance(totals, packed):
        piece_in, piece_seg, piece_len, piece_cot = packed

        def forward(values, weights):
            return layer(values, weights, piece_seg, piece_len)
        result, pullback = jax.vjp(forward, piece_in, params)
        grad_in, grad_weights = pullback(piece_cot)
        return (jax.tree.map(jnp.add, totals, grad_weights), (result.astype(jnp.bfloat16), grad_in))
    totals, (results, grads_in) = lax.scan(advance, jax.tree.map(jnp.zeros_like, params), (block_inputs, block_segs, block_lens, block_cots))
    return (results.reshape(TOKENS, D), grads_in.reshape(TOKENS, D), totals[0], totals[1], totals[2], totals[3], totals[4], totals[5], totals[6], totals[7], totals[8], totals[9], totals[10], totals[11], totals[12], totals[13], totals[14])
```

```python
from functools import partial

import jax
import jax.numpy as jnp
from jax import lax
from jax.experimental import pallas as pl
from jax.experimental.pallas import tpu as pltpu
from jax.sharding import PartitionSpec as P

HD = 64
EPS = 1e-12
NEGATIVE = -1e30
AXES = ("rows", "tp")
BF = jnp.bfloat16
F32 = jnp.float32
VMEM_LIMIT = 62 * 1024 * 1024
NN = (((1,), (0,)), ((), ()))
NT = (((1,), (1,)), ((), ()))
TN = (((0,), (0,)), ((), ()))


def mm(left, right, dims=NN):
    return lax.dot_general(left, right, dims, preferred_element_type=F32)


def rows_ds(start, size):
    return pl.ds(pl.multiple_of(start, size), size)


def call(body, out_shape, in_specs, scratch, name, flops, moved, out_specs=None):
    return pl.pallas_call(
        body,
        out_shape=out_shape,
        in_specs=in_specs,
        out_specs=out_specs,
        scratch_shapes=scratch,
        name=name,
        cost_estimate=pl.CostEstimate(flops=flops, bytes_accessed=moved, transcendentals=0),
        compiler_params=pltpu.CompilerParams(vmem_limit_bytes=VMEM_LIMIT),
    )


def vmem():
    return pl.BlockSpec(memory_space=pltpu.VMEM)


def smem():
    return pl.BlockSpec(memory_space=pltpu.SMEM)


def anywhere():
    return pl.BlockSpec(memory_space=pl.ANY)


def shape(dims, dtype=BF):
    return jax.ShapeDtypeStruct(dims, dtype)


def mask_bias(kc_ref, qc_ref, qb, kb, blk):
    match = kc_ref[rows_ds(kb * blk, blk), :] == qc_ref[qb]
    row = lax.broadcasted_iota(jnp.int32, (blk, blk), 0) + kb * blk
    col = lax.broadcasted_iota(jnp.int32, (blk, blk), 1) + qb * blk
    return jnp.where(match | (row == col), 0.0, NEGATIVE)


def attn_fwd_body(
    meta, xa, xb, w0, w1, w2, w3, bias, kc, qc,
    q_out, k_out, v_out, ctx_out, lse_out, own_out, oth_out, aw,
    m_s, l_s, acc_s,
):
    blk = kc.shape[1]
    half = xa.shape[0] // blk
    nb = 2 * half
    heads = q_out.shape[0]
    per = heads // 2
    quarter = w0.shape[1]
    chip = meta[1]
    for step, piece in enumerate((w0, w1, w2, w3)):
        for s in range(2):
            aw[s, rows_ds((chip ^ step) * quarter, quarter), :] = piece[s]
    for rb in range(nb):
        src = xa if rb < half else xb
        x = src[(rb % half) * blk:(rb % half + 1) * blk, :]
        for s in range(2):
            y = mm(x, aw[s, :, :640]) + bias[s, :, :640]
            rows = slice(rb * blk, (rb + 1) * blk)
            for h in range(per):
                one = s * per + h
                q_out[one, rows, :] = (y[:, h * HD:(h + 1) * HD].astype(BF) * 0.125).astype(BF)
                k_out[one, rows, :] = y[:, 192 + h * HD:192 + (h + 1) * HD].astype(BF)
                v_out[one, rows, :] = y[:, 384 + h * HD:384 + (h + 1) * HD].astype(BF)
    m_s[...] = jnp.full_like(m_s, NEGATIVE)
    l_s[...] = jnp.zeros_like(l_s)
    acc_s[...] = jnp.zeros_like(acc_s)

    def pair(i, carry):
        code = meta[2 + i]
        qb = code >> 2
        kb = code & 3
        bias_t = mask_bias(kc, qc, qb, kb, blk)
        for h in range(heads):
            keys = k_out[h, rows_ds(kb * blk, blk), :]
            qs = q_out[h, rows_ds(qb * blk, blk), :]
            vs = v_out[h, rows_ds(kb * blk, blk), :]
            st = mm(keys, qs, NT) + bias_t
            m_old = m_s[qb, h:h + 1, :]
            m_new = jnp.maximum(m_old, jnp.max(st, axis=0, keepdims=True))
            p = jnp.exp(st - m_new)
            alpha = jnp.exp(m_old - m_new)
            m_s[qb, h:h + 1, :] = m_new
            l_s[qb, h:h + 1, :] = alpha * l_s[qb, h:h + 1, :] + jnp.sum(p, axis=0, keepdims=True)
            acc_s[h, qb] = alpha * acc_s[h, qb] + mm(vs, p.astype(BF), TN)
        return carry

    lax.fori_loop(0, meta[0], pair, 0)
    for qb in range(nb):
        total = l_s[qb]
        lse_out[qb] = m_s[qb] + jnp.log(jnp.maximum(total, 1e-37))
        inv = 1.0 / total
        for h in range(heads):
            c = acc_s[h, qb] * inv[h:h + 1, :]
            ctx_out[h // per, qb * blk:(qb + 1) * blk, (h % per) * HD:(h % per + 1) * HD] = (
                c.T.astype(BF)
            )
    for rb in range(nb):
        rows = slice(rb * blk, (rb + 1) * blk)
        part = mm(ctx_out[0, rows, :], aw[0, :, 576:768], NT)
        part = part + mm(ctx_out[1, rows, :], aw[1, :, 576:768], NT)
        dst = slice((rb % half) * blk, (rb % half + 1) * blk)
        if rb < half:
            own_out[dst, :] = part
        else:
            oth_out[dst, :] = part.astype(BF)


def attn_bwd_body(
    meta, dal_a, dal_b, xa, xb, q_in, k_in, v_in, ctx_in, lse, aw, kc, qc,
    g0, g1, g2, g3, own_out, oth_out,
    do_s, delta_s, dqt_s, dk_s, dv_s, dqkv_s, g_s,
):
    blk = kc.shape[1]
    half = xa.shape[0] // blk
    nb = 2 * half
    heads = q_in.shape[0]
    per = heads // 2
    quarter = g0.shape[1] - 16
    chip = meta[1]
    ones = jnp.ones((8, HD), F32)
    for rb in range(nb):
        src = dal_a if rb < half else dal_b
        d = src[(rb % half) * blk:(rb % half + 1) * blk, :]
        rows = slice(rb * blk, (rb + 1) * blk)
        for s in range(2):
            dc = mm(d, aw[s, :, 576:768]).astype(BF)
            prod = dc.astype(F32) * ctx_in[s, rows, :].astype(F32)
            for h in range(per):
                one = s * per + h
                do_s[one, rows, :] = dc[:, h * HD:(h + 1) * HD]
                row = lax.dot_general(
                    ones, prod[:, h * HD:(h + 1) * HD], NT,
                    precision=lax.Precision.HIGHEST, preferred_element_type=F32,
                )
                delta_s[rb, one:one + 1, :] = row[0:1, :]
    dqt_s[...] = jnp.zeros_like(dqt_s)
    dk_s[...] = jnp.zeros_like(dk_s)
    dv_s[...] = jnp.zeros_like(dv_s)

    def pair(i, carry):
        code = meta[2 + i]
        qb = code >> 2
        kb = code & 3
        bias_t = mask_bias(kc, qc, qb, kb, blk)
        krows = rows_ds(kb * blk, blk)
        qrows = rows_ds(qb * blk, blk)
        for h in range(heads):
            keys = k_in[h, krows, :]
            qs = q_in[h, qrows, :]
            do = do_s[h, qrows, :]
            st = mm(keys, qs, NT) + bias_t
            p = jnp.exp(st - lse[qb, h:h + 1, :])
            dp = mm(v_in[h, krows, :], do, NT)
            ds = (p * (dp - delta_s[qb, h:h + 1, :])).astype(BF)
            dv_s[h, krows, :] += mm(p.astype(BF), do)
            dk_s[h, krows, :] += mm(ds, qs)
            dqt_s[h, qb] += mm(keys, ds, TN)
        return carry

    lax.fori_loop(0, meta[0], pair, 0)
    for h in range(heads):
        s, lane = h // per, (h % per) * HD
        for rb in range(nb):
            rows = slice(rb * blk, (rb + 1) * blk)
            dqkv_s[s, rows, lane:lane + HD] = (dqt_s[h, rb] * 0.125).T.astype(BF)
            dqkv_s[s, rows, 192 + lane:192 + lane + HD] = dk_s[h, rows, :].astype(BF)
            dqkv_s[s, rows, 384 + lane:384 + lane + HD] = dv_s[h, rows, :].astype(BF)
    n = xa.shape[0]
    for s in range(2):
        g = mm(xa[...], dqkv_s[s, :n, :576], TN) + mm(xb[...], dqkv_s[s, n:, :576], TN)
        g_s[:, :576] = g.astype(BF)
        g = mm(dal_a[...], ctx_in[s, :n, :], TN) + mm(dal_b[...], ctx_in[s, n:, :], TN)
        g_s[:, 576:768] = g.astype(BF)
        total = jnp.sum(dqkv_s[s, :, :576].astype(F32), axis=0, keepdims=True)
        high = total.astype(BF).astype(F32)
        low = total - high
        pad = jnp.zeros((7, 576), F32)
        extra = jnp.concatenate([high, pad, low, pad], axis=0).astype(BF)
        for step, out in enumerate((g0, g1, g2, g3)):
            out[s, :quarter, :] = g_s[rows_ds((chip ^ step) * quarter, quarter), :]
            out[s, quarter:, :] = jnp.zeros((16, 768), BF)
            out[s, quarter:, :576] = extra
    for rb in range(nb):
        rows = slice(rb * blk, (rb + 1) * blk)
        dx = mm(dqkv_s[0, rows, :576], aw[0, :, :576], NT)
        dx = dx + mm(dqkv_s[1, rows, :576], aw[1, :, :576], NT)
        dst = slice((rb % half) * blk, (rb % half + 1) * blk)
        if rb < half:
            own_out[dst, :] = dx
        else:
            oth_out[dst, :] = dx.astype(BF)


def norm_forward(values, gain, shift):
    centre = values - jnp.mean(values, axis=-1, keepdims=True)
    inverse = lax.rsqrt(jnp.mean(centre * centre, axis=-1, keepdims=True) + EPS)
    normed = centre * inverse
    return normed * gain + shift, normed, inverse


def norm_backward(upstream, normed, inverse, gain):
    scaled = upstream * gain
    inner = scaled - jnp.mean(scaled, axis=-1, keepdims=True)
    inner = inner - normed * jnp.mean(scaled * normed, axis=-1, keepdims=True)
    return inner * inverse


def column_sum(values):
    return jnp.sum(values, axis=0, keepdims=True)


def ffn_body(
    meta, part_a, part_b, x, dy, vecs, upb, own_w1, own_w2,
    b0, b1, b2, b3, b4, b5, b6, b7,
    out, da_out, dal_out, k0, k1, k2, k3, s0, s1, s2, s3,
    w1, w2, h1_s, u_s, n1_s, r1_s, acc_s, act_s, gp_s, st1, st2, extra_s, sem_in, sem_out,
):
    tokens = x.shape[0]
    blk = 256
    nb = tokens // blk
    piece = meta[1] * 2 + meta[18]
    chip, core = meta[1], meta[18]
    bufs = (b0, b1, b2, b3, b4, b5, b6, b7)
    size = 96
    copies = [[], [], [], []]
    for which, (src, dst) in enumerate(((own_w1, w1), (own_w2, w2))):
        copies[0].append(pltpu.make_async_copy(src, dst.at[0], sem_in.at[which]))
    at = 2
    for slot in range(1, 4):
        for step in range(8):
            rows = rows_ds((piece ^ step) * size, size)
            for which, dst in enumerate((w1, w2)):
                copies[slot].append(
                    pltpu.make_async_copy(
                        bufs[step].at[slot - 1, pl.ds(which * size, size), :],
                        dst.at[slot, rows, :],
                        sem_in.at[at],
                    )
                )
                at += 1
    for group in copies:
        for copy in group:
            copy.start()
    gain1, shift1, gain2, shift2 = vecs[0:1, :], vecs[1:2, :], vecs[2:3, :], vecs[3:4, :]
    bias_o, bias_d = vecs[4:5, :], vecs[5:6, :]
    for rb in range(nb):
        rows = slice(rb * blk, (rb + 1) * blk)
        a = x[rows, :].astype(F32) + (part_a[rows, :] + part_b[rows, :].astype(F32)) + bias_o
        h1, n1, r1 = norm_forward(a, gain1, shift1)
        h1_s[rows, :] = h1
        u_s[rows, :] = h1.astype(BF)
        n1_s[rows, :] = n1
        r1_s[rows, :] = jnp.broadcast_to(r1, (blk, 128))
        acc_s[rows, :] = h1 + bias_d
    for slot in range(4):
        for copy in copies[slot]:
            copy.wait()
        for rb in range(nb):
            rows = slice(rb * blk, (rb + 1) * blk)
            z = mm(u_s[rows, :], w1[slot]) + upb[slot]
            half_erf = 0.5 * lax.erf(z * 0.7071067811865476) + 0.5
            act = (z * half_erf).astype(BF)
            act_s[slot, rows, :] = act
            gp_s[slot, rows, :] = half_erf + z * (0.3989422804014327 * jnp.exp(-0.5 * z * z))
            acc_s[rows, :] += mm(act, w2[slot])
    sums = [jnp.zeros((1, 768), F32) for _ in range(3)]
    for rb in range(nb):
        rows = slice(rb * blk, (rb + 1) * blk)
        result, n2, r2 = norm_forward(acc_s[rows, :], gain2, shift2)
        out[rows, :] = result.astype(BF)
        up = dy[rows, :].astype(F32)
        dc = norm_backward(up, n2, r2, gain2)
        sums[0] = sums[0] + column_sum(up * n2)
        sums[1] = sums[1] + column_sum(up)
        sums[2] = sums[2] + column_sum(dc)
        acc_s[rows, :] = dc
        dal_out[rows, :] = dc.astype(BF)
    keep, send = (k0, k1, k2, k3), (s0, s1, s2, s3)
    outs = []
    at = 0
    up_sums = []
    for slot in range(4):
        total = jnp.zeros((1, 768), F32)
        for rb in range(nb):
            rows = slice(rb * blk, (rb + 1) * blk)
            dz = mm(dal_out[rows, :], w2[slot], NT) * gp_s[slot, rows, :]
            total = total + column_sum(dz)
            gp_s[slot, rows, :] = dz
        up_sums.append(total)
        dzl = gp_s[slot].astype(BF)
        st2[slot] = mm(act_s[slot], dal_out[...], TN).astype(BF)
        st1[slot] = mm(u_s[...], dzl, TN).astype(BF)
        for which, stage in enumerate((st1, st2)):
            for step in range(4):
                for side, dst in enumerate((keep[step], send[step])):
                    p = ((chip ^ step) * 2) + (core ^ side)
                    copy = pltpu.make_async_copy(
                        stage.at[slot, rows_ds(p * size, size), :],
                        dst.at[slot, pl.ds(which * size, size), :],
                        sem_out.at[at],
                    )
                    at += 1
                    copy.start()
                    outs.append(copy)
        for rb in range(nb):
            rows = slice(rb * blk, (rb + 1) * blk)
            acc_s[rows, :] += mm(dzl[rows, :], w1[slot], NT)
    for _ in range(3):
        sums.append(jnp.zeros((1, 768), F32))
    for rb in range(nb):
        rows = slice(rb * blk, (rb + 1) * blk)
        dh = acc_s[rows, :]
        n1 = n1_s[rows, :]
        da = norm_backward(dh, n1, r1_s[rows, 0:1], gain1)
        sums[3] = sums[3] + column_sum(dh * n1)
        sums[4] = sums[4] + column_sum(dh)
        sums[5] = sums[5] + column_sum(da)
        da_out[rows, :] = da
        dal_out[rows, :] = da.astype(BF)
    for slot in range(4):
        full = jnp.concatenate(sums + [up_sums[slot], jnp.zeros((1, 768), F32)], axis=0)
        high = full.astype(BF).astype(F32)
        extra_s[slot] = jnp.concatenate([high, full - high], axis=0).astype(BF)
    for step in range(4):
        for dst in (keep[step], send[step]):
            copy = pltpu.make_async_copy(
                extra_s, dst.at[:, pl.ds(2 * size, 16), :], sem_out.at[at]
            )
            at += 1
            copy.start()
            outs.append(copy)
    for copy in outs:
        copy.wait()


def sum_body(*refs):
    out = refs[-1]
    total = refs[0][...].astype(F32)
    for ref in refs[1:-1]:
        total = total + ref[...].astype(F32)
    rows = out.shape[1] - 16
    out[:, :rows, :] = total[:, :rows, :].astype(BF)
    full = total[:, rows:rows + 8, :] + total[:, rows + 8:, :]
    high = full.astype(BF).astype(F32)
    out[:, rows:rows + 8, :] = high.astype(BF)
    out[:, rows + 8:, :] = (full - high).astype(BF)


def add_pieces(parts, name):
    slots, rows, cols = parts[0].shape
    spec = pl.BlockSpec((1, rows, cols), lambda i: (i, 0, 0))
    return pl.pallas_call(
        sum_body,
        grid=(slots,),
        in_specs=[spec] * len(parts),
        out_specs=spec,
        out_shape=shape((slots, rows, cols)),
        name=name,
        cost_estimate=pl.CostEstimate(
            flops=slots * rows * cols * len(parts),
            bytes_accessed=slots * rows * cols * 2 * (len(parts) + 1),
            transcendentals=0,
        ),
    )(*parts)


def place_body(meta, *refs):
    groups = (len(refs)) - 8
    piece = meta[1] * 2 + meta[18]
    for step in range(8):
        rows = rows_ds((piece ^ step) * 96, 96)
        for g in range(groups):
            refs[8 + g][rows, :] = refs[step][g * 96:(g + 1) * 96, :].astype(F32)


def per_device(
    inputs, segments, row_length, query_weight, query_bias, key_weight, value_weight, value_bias,
    output_weight, output_bias, attn_gain, attn_shift, up_weight, up_bias, down_weight, down_bias,
    ffn_gain, ffn_shift, cotangent,
):
    n_rows, n_tp = lax.axis_size("rows"), lax.axis_size("tp")
    half, width = inputs.shape
    seq = segments.shape[1]
    blk = 256
    nb = seq // blk
    r_at, z_at = lax.axis_index("rows"), lax.axis_index("tp")
    core, chip = r_at & 1, (r_at >> 1) & 3

    def permute(value, target):
        pairs = []
        for r in range(n_rows):
            for z in range(n_tp):
                r2, z2 = target(r, z)
                pairs.append((r * n_tp + z, r2 * n_tp + z2))
        return lax.ppermute(value, AXES, pairs)

    def flip(bit):
        return lambda r, z: (r ^ bit, z)

    def swap(r, z):
        return (r & ~1) | (z & 1), (z & ~1) | (r & 1)

    def shift_by(k):
        return lambda r, z: (r, (z + k) % n_tp)

    def three_rows(vector):
        parts = []
        rest = vector
        for _ in range(3):
            top = rest.astype(BF)
            parts.append(top)
            rest = rest - top.astype(F32)
        return jnp.concatenate([jnp.stack(parts), jnp.zeros((13, width), BF)], axis=0)

    quarter = width // 4
    aw_own = jnp.concatenate([query_weight, key_weight, value_weight, output_weight.T], axis=1)
    bias_vec = jnp.concatenate(
        [query_bias, jnp.zeros_like(query_bias), value_bias, jnp.zeros_like(value_bias)]
    )
    aw_piece = jnp.concatenate(
        [lax.dynamic_slice_in_dim(aw_own, chip * quarter, quarter, 0), three_rows(bias_vec)], axis=0
    )
    first = permute(aw_piece, lambda r, z: (r, (z + 2 * (r & 1)) % n_tp))
    second = permute(aw_piece, lambda r, z: (r, (z + 2 * (r & 1) + 1) % n_tp))
    x_own = permute(inputs, swap)
    places = jnp.arange(seq, dtype=jnp.int32)[None, :]
    codes = jnp.concatenate(
        [segments, jnp.where(places < row_length[:, None], segments, -1)], axis=0
    )
    codes_other = permute(codes, flip(1))
    aw_mine = jnp.stack([first[:quarter], second[:quarter]])
    aw_pieces = [aw_mine] + [permute(aw_mine, flip(2 * m)) for m in (1, 2, 3)]
    bias = jnp.stack([first[quarter:], second[quarter:]]).astype(F32)
    bias = jnp.sum(bias[:, :3], axis=1, keepdims=True)
    x_oth = permute(x_own, flip(1))

    piece = chip * 2 + core
    size = width // 8
    fw_piece = jnp.concatenate(
        [
            lax.dynamic_slice_in_dim(up_weight, piece * size, size, 0),
            lax.dynamic_slice_in_dim(down_weight, piece * size, size, 0),
            three_rows(up_bias),
        ],
        axis=0,
    )
    fw_z = [permute(fw_piece, shift_by(k)) for k in (1, 2, 3)]
    fw_mine = jnp.stack([part[:2 * size] for part in fw_z])
    fw_plane = [fw_mine] + [permute(fw_mine, flip(2 * m)) for m in (1, 2, 3)]
    fw_all = []
    for part in fw_plane:
        fw_all += [part, permute(part, flip(1))]
    upb = jnp.stack([part[2 * size:2 * size + 3] for part in fw_z]).astype(F32)
    upb = jnp.concatenate([up_bias[None, None], jnp.sum(upb, axis=1, keepdims=True)], axis=0)
    dy = permute(cotangent, swap)

    mine = jnp.where((z_at & 1) == core, codes, codes_other)
    here = lax.dynamic_index_in_dim(mine.reshape(2, 2, seq), z_at >> 1, 1, keepdims=False)
    turned = jnp.concatenate([here[:, half:], here[:, :half]], axis=1)
    here = jnp.where(core == 0, here, turned)
    q_code, k_code = here[0], here[1]
    q_low = jnp.min(q_code.reshape(nb, blk), axis=1)
    q_high = jnp.max(q_code.reshape(nb, blk), axis=1)
    live = jnp.where(k_code < 0, 1 << 20, k_code).reshape(nb, blk)
    k_low = jnp.min(live, axis=1)
    k_high = jnp.max(k_code.reshape(nb, blk), axis=1)
    active = (k_low[None, :] <= q_high[:, None]) & (k_high[None, :] >= q_low[:, None])
    active = (active | jnp.eye(nb, dtype=bool)).reshape(-1)
    order = jnp.cumsum(active.astype(jnp.int32)) - 1
    slots = jnp.where(active, order, nb * nb)
    numbers = jnp.arange(nb * nb, dtype=jnp.int32)
    listed = jnp.sum(
        jnp.where(slots[None, :] == numbers[:, None], numbers[None, :], 0), axis=1
    )
    meta = jnp.concatenate(
        [
            jnp.stack([jnp.sum(active.astype(jnp.int32)), chip]),
            listed,
            jnp.stack([core, core]),
        ]
    ).astype(jnp.int32)
    kc = jnp.broadcast_to(k_code.astype(F32)[:, None], (seq, blk))
    qc = q_code.astype(F32).reshape(nb, 1, blk)

    heads = 2 * query_weight.shape[1] // HD
    per_head = shape((heads, seq, HD))
    (q_h, k_h, v_h, ctx, lse, part_own, part_oth, aw) = call(
        attn_fwd_body,
        (
            per_head, per_head, per_head, shape((2, seq, 192)), shape((nb, 8, blk), F32),
            shape((half, width), F32), shape((half, width)), shape((2, width, width)),
        ),
        [smem()] + [vmem()] * 9,
        [
            pltpu.VMEM((nb, 8, blk), F32),
            pltpu.VMEM((nb, 8, blk), F32),
            pltpu.VMEM((heads, nb, HD, blk), F32),
        ],
        "attn_fwd", 6 << 30, 16 << 20, (vmem(),) * 8,
    )(meta, x_own, x_oth, *aw_pieces, bias, kc, qc)
    part_in = permute(part_oth, flip(1))

    zero = jnp.zeros_like(attn_gain)
    vecs = jnp.stack(
        [attn_gain, attn_shift, ffn_gain, ffn_shift, output_bias, down_bias, zero, zero]
    )
    grads = shape((4, 2 * size + 16, width))
    outs = call(
        ffn_body,
        (shape((half, width)), shape((half, width), F32), shape((half, width))) + (grads,) * 8,
        [smem()] + [vmem()] * 6 + [anywhere()] * 10,
        [
            pltpu.VMEM((4, width, width), BF),
            pltpu.VMEM((4, width, width), BF),
            pltpu.VMEM((half, width), F32),
            pltpu.VMEM((half, width), BF),
            pltpu.VMEM((half, width), F32),
            pltpu.VMEM((half, 128), F32),
            pltpu.VMEM((half, width), F32),
            pltpu.VMEM((4, half, width), BF),
            pltpu.VMEM((4, half, width), F32),
            pltpu.VMEM((4, width, width), BF),
            pltpu.VMEM((4, width, width), BF),
            pltpu.VMEM((4, 16, width), BF),
            pltpu.SemaphoreType.DMA((50,)),
            pltpu.SemaphoreType.DMA((72,)),
        ],
        "ffn", 15 << 30, 32 << 20, (vmem(),) * 3 + (anywhere(),) * 8,
    )(meta, part_own, part_in, x_own, dy, vecs, upb, up_weight, down_weight, *fw_all)
    layer_rows, da, dal = outs[:3]
    keep, send = outs[3:7], outs[7:]
    dal_oth = permute(dal, flip(1))
    layer_out = permute(layer_rows, swap)

    came = [permute(part, flip(1)) for part in send]
    chip_sum = [None] + [add_pieces((keep[m], came[m]), f"ffn_core_{m}") for m in (1, 2, 3)]
    plane = [permute(chip_sum[m], flip(2 * m)) for m in (1, 2, 3)]
    ffn_sum = add_pieces((keep[0], came[0], *plane), "ffn_plane")
    bit = 8
    while bit < n_rows:
        ffn_sum = add_pieces((ffn_sum, permute(ffn_sum, flip(bit))), f"ffn_wide_{bit}")
        bit *= 2
    ffn_back = [permute(ffn_sum[k], shift_by(-k)) for k in (1, 2, 3)]
    ffn_total = add_pieces(
        (ffn_sum[0][None], *[part[None] for part in ffn_back]), "ffn_tp"
    )[0]
    ffn_mine = ffn_total[:2 * size]
    ffn_planes = [ffn_mine] + [permute(ffn_mine, flip(2 * m)) for m in (1, 2, 3)]
    ffn_all = []
    for part in ffn_planes:
        ffn_all += [part, permute(part, flip(1))]
    full = shape((width, width), F32)
    up_grad, down_grad = call(
        place_body, (full, full), [smem()] + [vmem()] * 8, [], "ffn_place", 1 << 20, 8 << 20,
        (vmem(),) * 2,
    )(meta, *ffn_all)
    small = ffn_total[2 * size:].astype(F32)
    small = small[:8] + small[8:]

    quart = shape((2, quarter + 16, width))
    g0, g1, g2, g3, dx_own, dx_oth = call(
        attn_bwd_body,
        (quart,) * 4 + (shape((half, width), F32), shape((half, width))),
        [smem()] + [vmem()] * 12,
        [
            pltpu.VMEM((heads, seq, HD), BF),
            pltpu.VMEM((nb, 8, blk), F32),
            pltpu.VMEM((heads, nb, HD, blk), F32),
            pltpu.VMEM((heads, seq, HD), F32),
            pltpu.VMEM((heads, seq, HD), F32),
            pltpu.VMEM((2, seq, width), BF),
            pltpu.VMEM((width, width), BF),
        ],
        "attn_bwd", 12 << 30, 24 << 20, (vmem(),) * 6,
    )(meta, dal, dal_oth, x_own, x_oth, q_h, k_h, v_h, ctx, lse, aw, kc, qc)
    dx_in = permute(dx_oth, flip(1))
    att_plane = [permute(g, flip(2 * m)) for m, g in ((1, g1), (2, g2), (3, g3))]
    input_rows = da + (dx_own + dx_in.astype(F32))
    input_grad = permute(input_rows.astype(BF), swap).astype(F32)
    att_sum = add_pieces((g0, *att_plane), "att_plane")
    bit = 8
    while bit < n_rows:
        att_sum = add_pieces((att_sum, permute(att_sum, flip(bit))), f"att_wide_{bit}")
        bit *= 2
    back_a = permute(att_sum[0], lambda r, z: (r, (z - 2 * (r & 1)) % n_tp))
    back_b = permute(att_sum[1], lambda r, z: (r, (z - 2 * (r & 1) - 1) % n_tp))
    att_half = add_pieces((back_a[None], back_b[None]), "att_tp")
    att_total = add_pieces((att_half, permute(att_half, flip(1))), "att_core")[0]
    att_mine = lax.dynamic_slice_in_dim(att_total, core * size, size, 0)
    att_planes = [att_mine] + [permute(att_mine, flip(2 * m)) for m in (1, 2, 3)]
    att_all = []
    for part in att_planes:
        att_all += [part, permute(part, flip(1))]
    att_grad = call(
        place_body, (full,), [smem()] + [vmem()] * 8, [], "att_place", 1 << 20, 4 << 20,
        (vmem(),),
    )(meta, *att_all)[0]
    tiny = att_total[quarter:].astype(F32)
    tiny = tiny[0] + tiny[8]
    cols = query_weight.shape[1]
    return (
        layer_out,
        input_grad,
        att_grad[:, :cols],
        tiny[:cols],
        att_grad[:, cols:2 * cols],
        att_grad[:, 2 * cols:3 * cols],
        tiny[2 * cols:3 * cols],
        att_grad[:, 3 * cols:].T,
        small[5],
        small[3],
        small[4],
        up_grad,
        small[6],
        down_grad,
        small[2],
        small[0],
        small[1],
    )


def solution(mesh):
    tokens = P(("rows", "tp"), None)
    by_col, by_row, vec, whole = P(None, "tp"), P("tp", None), P("tp"), P()
    in_specs = (
        tokens, P("rows", None), P("rows"), by_col, vec, by_col, by_col, vec, by_row, whole, whole,
        whole, by_col, vec, by_row, whole, whole, whole, tokens,
    )
    out_specs = (
        tokens, tokens, by_col, vec, by_col, by_col, vec, by_row, whole, whole, whole, by_col, vec,
        by_row, whole, whole, whole,
    )
    return jax.shard_map(
        per_device, mesh=mesh, in_specs=in_specs, out_specs=out_specs, check_vma=False
    )
```
